32 devices in a mesh: ha: 4 (over z), wa: 8 (over y, x, core).
Axes of the slice: x: 2, y: 2, z: 4, core: 2. Of those that a mesh axis runs over, the one named last changes fastest.
Arguments:
- tokens: bfloat16 [32, 128, 512], P('ha', 'wa'), may hold values from -6 to 6
- cotangent: bfloat16 [32, 128, 512], P('ha', 'wa'), may hold values from -6 to 6
- state_in: float32 [32, 128, 16], P('ha', 'wa'), may hold values from -0.25 to 0.25
- state_out: float32 [32, 128, 16], P('ha', 'wa'), may hold values from -0.25 to 0.25
- width_decay: float32 [32, 128, 8], P('ha', 'wa'), may hold values from -1.6 to 0
- height_decay: float32 [32, 128, 8], P('ha', 'wa'), may hold values from -1.6 to 0
Outputs:
- tokens_grad: float32 [32, 128, 512], P('ha', 'wa')
- state_in_grad: float32 [32, 128, 16], P('ha', 'wa')
- state_out_grad: float32 [32, 128, 16], P('ha', 'wa')
- width_decay_grad: float32 [32, 128, 8], P('ha', 'wa')
- height_decay_grad: float32 [32, 128, 8], P('ha', 'wa')
The draws below stay inside these ranges and needn't reach their ends.
All inputs are finite; a program needn't handle non-finite values.
Results may differ from the reference program's by a relative error of at most 0.0003.
Values sent between devices are 32-bit elements; how exact they have to be, the bound alone decides.
A program may use at most 128 MiB of HBM per device.

```python
import jax
import jax.numpy as jnp
from jax import lax

D = 512
G = 8
N = 16
HEIGHT = 32
WIDTH = 128


def decay_logs(key, direction, sequence_length):
    key_list = jax.random.split(key, 7)
    fast_count = jax.random.randint(key_list[0], (), 2, 5)
    ranking = jax.random.permutation(key_list[1], G)
    is_fast = ranking < fast_count
    slow_rate = jax.random.uniform(key_list[2], (G,), jnp.float32, 0.1, 0.5) / sequence_length
    fast_rate = jnp.exp(jax.random.uniform(key_list[3], (G,), jnp.float32, jnp.log(1.0 / 50.0), jnp.log(1.0 / 30.0)))
    cluster_decay_rate = jnp.where(is_fast, fast_rate, slow_rate)
    texture_jitter = jnp.exp(jax.random.uniform(key_list[4], (HEIGHT, WIDTH, G), jnp.float32, jnp.log(0.5), jnp.log(2.0)))
    position_indices = jax.random.randint(key_list[5], (3,), 0, sequence_length)
    loss_values = jax.random.uniform(key_list[6], (3,), jnp.float32, 0.22, 0.51)
    spike_stripe_row = jnp.sum(loss_values[:, None] * (jnp.arange(sequence_length)[None, :] == position_indices[:, None]).astype(jnp.float32), axis=0)
    if direction == 1:
        spike_lattice = spike_stripe_row[None, :, None]
    else:
        spike_lattice = spike_stripe_row[:, None, None]
    return (-(cluster_decay_rate * texture_jitter + spike_lattice)).astype(jnp.float32)


def draw_width_decay(key, part):
    return decay_logs(jax.random.fold_in(key, 11), 1, WIDTH)


def draw_height_decay(key, part):
    return decay_logs(jax.random.fold_in(key, 23), 0, HEIGHT)


def steps_of(rng, shape, cuts, least, high):
    loudness = 1.0
    for axis_at, blocks in cuts:
        draws = jax.random.uniform(jax.random.fold_in(jax.random.fold_in(rng, 6), axis_at), (blocks,), jnp.float32, least / len(cuts), high / len(cuts))
        loudness = loudness * jnp.repeat(jnp.exp(draws), shape[axis_at] // blocks).reshape((-1,) + (1,) * (len(shape) - 1 - axis_at))
    return loudness


def centred(own_key, extent, scale, bound, cuts=(), kind=jnp.bfloat16):
    level = steps_of(own_key, extent, cuts, -0.22, 0.18) if cuts else 1.0
    entries = jax.random.normal(own_key, extent, jnp.float32) * scale * level
    return jnp.minimum(jnp.maximum(entries, -bound), bound).astype(kind)


def setup_inputs(seed: int = 0) -> dict:
    key_of = jax.random.split(jax.random.key(seed), 7)
    return {
        "tokens": centred(key_of[0], (HEIGHT, WIDTH, D), 1.0, 6.0, ((0, 4), (1, 8))),
        "cotangent": centred(key_of[1], (HEIGHT, WIDTH, D), 1.0, 6.0, ((0, 4), (1, 8))),
        "state_in": centred(key_of[2], (HEIGHT, WIDTH, N), 0.03125, 0.25, ((0, 4), (1, 8)), jnp.float32),
        "state_out": centred(key_of[3], (HEIGHT, WIDTH, N), 0.03125, 0.25, ((0, 4), (1, 8)), jnp.float32),
        "width_decay": draw_width_decay(jax.random.fold_in(key_of[6], 71), 0),
        "height_decay": draw_height_decay(jax.random.fold_in(key_of[6], 71), 0),
    }


def advance(carry, item):
    rate, term = item
    carry = rate * carry + term
    return carry, carry


def retreat(carry, item):
    rate, term = item
    total = term + carry
    return rate * total, total


def slab_grads(values, grads_out, log_width, log_height, state_in, state_out):
    width_rate = jnp.exp(log_width)[:, :, None, :]
    height_rate = jnp.exp(log_height)[:, :, None, :]
    slab_width = values.shape[2]
    driven = state_in[:, :, :, None] * values[:, :, None, :]
    zero_rows = jnp.zeros((HEIGHT, N, slab_width), jnp.float32)
    zero_cols = jnp.zeros((WIDTH, N, slab_width), jnp.float32)
    ignored, states = lax.scan(advance, zero_rows, (jnp.swapaxes(width_rate, 0, 1), jnp.swapaxes(driven, 0, 1)))
    states = jnp.swapaxes(states, 0, 1)
    ignored, totals = lax.scan(advance, zero_cols, (height_rate, states))
    seeded = state_out[:, :, :, None] * grads_out[:, :, None, :]
    ignored, col_grad = lax.scan(retreat, zero_cols, (height_rate, seeded), reverse=True)
    earlier_rows = jnp.concatenate([jnp.zeros_like(totals[:1]), totals[:-1]], axis=0)
    height_grad = jnp.exp(log_height) * jnp.sum(col_grad * earlier_rows, axis=2)
    out_grad = jnp.sum(totals * grads_out[:, :, None, :], axis=3)
    ignored, row_grad = lax.scan(retreat, zero_rows, (jnp.swapaxes(width_rate, 0, 1), jnp.swapaxes(col_grad, 0, 1)), reverse=True)
    row_grad = jnp.swapaxes(row_grad, 0, 1)
    earlier_cols = jnp.concatenate([jnp.zeros_like(states[:, :1]), states[:, :-1]], axis=1)
    width_grad = jnp.exp(log_width) * jnp.sum(row_grad * earlier_cols, axis=2)
    in_grad = jnp.sum(row_grad * values[:, :, None, :], axis=3)
    token_grad = jnp.sum(row_grad * state_in[:, :, :, None], axis=2)
    return token_grad, in_grad, out_grad, width_grad, height_grad


def reference(tokens, cotangent, state_in, state_out, width_decay, height_decay):
    slab_width = 8
    count = D // slab_width
    group_width = D // G

    def one_slab(carry, number):
        offset = (number * slab_width).astype(jnp.int32)
        values = lax.dynamic_slice_in_dim(tokens, offset, slab_width, 2).astype(jnp.float32)
        grads_out = lax.dynamic_slice_in_dim(cotangent, offset, slab_width, 2).astype(jnp.float32)
        group = (offset // group_width).astype(jnp.int32)
        log_width = jnp.broadcast_to(lax.dynamic_slice_in_dim(width_decay, group, 1, 2), (HEIGHT, WIDTH, slab_width))
        log_height = jnp.broadcast_to(lax.dynamic_slice_in_dim(height_decay, group, 1, 2), (HEIGHT, WIDTH, slab_width))
        token_grad, in_grad, out_grad, width_grad, height_grad = slab_grads(values, grads_out, log_width, log_height, state_in, state_out)
        return (carry[0] + in_grad, carry[1] + out_grad), (token_grad, jnp.sum(width_grad, axis=2), jnp.sum(height_grad, axis=2))

    start = (jnp.zeros((HEIGHT, WIDTH, N), jnp.float32), jnp.zeros((HEIGHT, WIDTH, N), jnp.float32))
    sums, slabs = lax.scan(one_slab, start, jnp.arange(count, dtype=jnp.int32))
    token_parts, width_parts, height_parts = slabs
    tokens_grad = jnp.transpose(token_parts, (1, 2, 0, 3)).reshape(HEIGHT, WIDTH, D)
    width_decay_grad = jnp.transpose(jnp.sum(width_parts.reshape(G, group_width // slab_width, HEIGHT, WIDTH), axis=1), (1, 2, 0))
    height_decay_grad = jnp.transpose(jnp.sum(height_parts.reshape(G, group_width // slab_width, HEIGHT, WIDTH), axis=1), (1, 2, 0))
    return tokens_grad, sums[0], sums[1], width_decay_grad, height_decay_grad
```

```python
import functools

import jax
import jax.numpy as jnp
from jax import lax
from jax.experimental import pallas as pl
from jax.experimental.pallas import tpu as pltpu
from jax.sharding import PartitionSpec as P

MESH = pl.DeviceIdType.MESH
F32 = jnp.float32


def kernel(
    ha,
    wa,
    x_in,
    cot_in,
    bt,
    ct,
    wl,
    hl,
    tok_out,
    in_out,
    so_out,
    wg_out,
    hg_out,
    x,
    cot,
    wr,
    hr,
    pw,
    ph,
    rpw,
    rph,
    eh0,
    rh0,
    oh0,
    ih0,
    eh1,
    rh1,
    oh1,
    ih1,
    ew0,
    rw0,
    ow0,
    iw0,
    ew1,
    rw1,
    ow1,
    iw1,
    states,
    grads,
    part,
    send,
    recv,
):
    rows, cols, channels = x_in.shape
    n = bt.shape[1]
    groups = wl.shape[1]
    gw = channels // groups
    split = ew0.shape[0] // rows
    chunk = channels // split
    per_w = rows * split // wa
    per_h = cols // ha
    me_h = lax.axis_index("ha")
    me_w = lax.axis_index("wa")
    place = {"ha": (me_h, ha, per_h), "wa": (me_w, wa, per_w)}

    barrier = pltpu.get_barrier_semaphore()
    for axis in ("ha", "wa"):
        me, count, per = place[axis]
        for d in range(1, count):
            pl.semaphore_signal(
                barrier, inc=1, device_id={axis: lax.rem(me + d, count)}, device_id_type=MESH
            )

    def copies(axis, k, source, target):
        me, count, per = place[axis]
        made = []
        for d in range(1, count):
            peer = lax.rem(me + d, count)
            made.append(
                pltpu.make_async_remote_copy(
                    src_ref=source(peer, per),
                    dst_ref=target(me, per),
                    send_sem=send.at[k, d],
                    recv_sem=recv.at[k, d],
                    device_id={axis: peer},
                    device_id_type=MESH,
                )
            )
        return made

    started = []

    def scatter(axis, k, ends, got):
        made = copies(
            axis, k, lambda peer, per: ends.at[pl.ds(peer * per, per)], lambda me, per: got.at[me]
        )
        for c in made:
            c.start()
        me, count, per = place[axis]
        got[me] = ends[pl.ds(me * per, per)]
        started.extend(made)
        return made

    def give_back(axis, k, result, first):
        made = copies(
            axis, k, lambda peer, per: result.at[peer], lambda me, per: first.at[pl.ds(me * per, per)]
        )
        for c in made:
            c.start()
        me, count, per = place[axis]
        first[pl.ds(me * per, per)] = result[me]
        started.extend(made)
        return made

    def arrive(made):
        for c in made:
            c.wait_recv()

    def put(buffer, i, value):
        for q in range(split):
            buffer[i * split + q] = value[:, q * chunk : (q + 1) * chunk]

    def take(buffer, i):
        return jnp.concatenate([buffer[i * split + q] for q in range(split)], axis=1)

    def chain(axis, got, product, result, backward):
        me, count, per = place[axis]
        order = range(count - 1, -1, -1) if backward else range(count)
        for p in range(per):
            current = jnp.zeros(got.shape[2:], F32)
            for s in order:
                result[s, p] = current
                current = product[s, p] * current + got[s, p]

    def onehot(shape, group_dim):
        g = lax.broadcasted_iota(jnp.int32, shape, group_dim) * gw
        c = lax.broadcasted_iota(jnp.int32, shape, 1 - group_dim)
        return jnp.where((c >= g) & (c < g + gw), 1.0, 0.0).astype(F32)

    def dot(a, b):
        return jnp.dot(a, b, precision=lax.Precision.HIGHEST, preferred_element_type=F32)

    spread = onehot((groups, channels), 0)
    hr[...] = dot(jnp.exp(hl[...]), spread).reshape(rows, cols, channels)
    wr[...] = dot(jnp.exp(wl[...]), spread).reshape(rows, cols, channels)
    x[...] = x_in[...].astype(F32)
    cot[...] = cot_in[...].astype(F32)
    whole = hr[0]
    for i in range(1, rows):
        whole = whole * hr[i]
    for j in range(cols):
        ph[j] = whole[j : j + 1]
    for i in range(rows):
        one = wr[i, 0:1, :]
        for j in range(1, cols):
            one = one * wr[i, j : j + 1, :]
        put(pw, i, one)

    eh0[...] = jnp.zeros_like(eh0)
    eh1[...] = jnp.zeros_like(eh1)

    def col_ends(t, unused):
        i = rows - 1 - t
        columns = ct[i]
        for j in range(cols):
            total = columns[:, j : j + 1] * cot[i, j : j + 1, :] + eh0[j]
            eh0[j] = hr[i, j : j + 1, :] * total
        return unused

    lax.fori_loop(0, rows, col_ends, 0)

    pl.semaphore_wait(barrier, ha + wa - 2)
    got_ph = scatter("ha", 8, ph, rph)
    out_h0 = scatter("ha", 0, eh0, rh0)

    def row_ends(i, unused):
        columns = bt[i]
        carry = columns[:, 0:1] * x[i, 0:1, :]
        for j in range(1, cols):
            carry = wr[i, j : j + 1, :] * carry + columns[:, j : j + 1] * x[i, j : j + 1, :]
        put(ew0, i, carry)
        return unused

    lax.fori_loop(0, rows, row_ends, 0)
    got_pw = scatter("wa", 9, pw, rpw)
    out_w0 = scatter("wa", 1, ew0, rw0)

    arrive(got_ph)
    arrive(out_h0)
    chain("ha", rh0, rph, oh0, True)
    back_h0 = give_back("ha", 4, oh0, ih0)
    arrive(got_pw)
    arrive(out_w0)
    chain("wa", rw0, rpw, ow0, False)
    back_w0 = give_back("wa", 5, ow0, iw0)

    arrive(back_h0)

    def backward(t, unused):
        i = rows - 1 - t
        columns = ct[i]
        carry = jnp.zeros((n, channels), F32)
        for j in range(cols - 1, -1, -1):
            grad = columns[:, j : j + 1] * cot[i, j : j + 1, :] + ih0[j]
            grads[i, j] = grad
            ih0[j] = hr[i, j : j + 1, :] * grad
            carry = wr[i, j : j + 1, :] * (grad + carry)
        put(ew1, i, carry)
        return unused

    lax.fori_loop(0, rows, backward, 0)
    out_w1 = scatter("wa", 2, ew1, rw1)

    arrive(back_w0)

    def forward(i, unused):
        columns = bt[i]
        carry = take(iw0, i)
        for j in range(cols):
            carry = wr[i, j : j + 1, :] * carry + columns[:, j : j + 1] * x[i, j : j + 1, :]
            states[i, j] = carry
            eh1[j] = hr[i, j : j + 1, :] * eh1[j] + carry
        return unused

    lax.fori_loop(0, rows, forward, 0)
    out_h1 = scatter("ha", 3, eh1, rh1)

    arrive(out_w1)
    chain("wa", rw1, rpw, ow1, True)
    back_w1 = give_back("wa", 6, ow1, iw1)
    arrive(out_h1)
    chain("ha", rh1, rph, oh1, False)
    back_h1 = give_back("ha", 7, oh1, ih1)

    lane = lax.broadcasted_iota(jnp.int32, (n, cols), 1)
    arrive(back_w1)

    def rows_done(i, unused):
        columns = bt[i]
        carry = take(iw1, i)
        sums = jnp.zeros((n, cols), F32)
        for j in range(cols - 1, -1, -1):
            grad = grads[i, j] + carry
            carry = wr[i, j : j + 1, :] * grad
            earlier = states[i, j - 1] if j else take(iw0, i)
            part[i, j : j + 1, :] = jnp.sum(grad * earlier, axis=0, keepdims=True)
            tok_out[i, j : j + 1, :] = jnp.sum(grad * columns[:, j : j + 1], axis=0, keepdims=True)
            sums = jnp.where(
                lane == j, jnp.sum(grad * x[i, j : j + 1, :], axis=1, keepdims=True), sums
            )
        in_out[i] = sums
        return unused

    lax.fori_loop(0, rows, rows_done, 0)
    gather = onehot((channels, groups), 1)
    wg_out[...] = jnp.exp(wl[...]) * dot(part[...].reshape(rows * cols, channels), gather)

    arrive(back_h1)

    def cols_done(i, unused):
        sums = jnp.zeros((n, cols), F32)
        for j in range(cols):
            earlier = ih1[j]
            part[i, j : j + 1, :] = jnp.sum(grads[i, j] * earlier, axis=0, keepdims=True)
            total = hr[i, j : j + 1, :] * earlier + states[i, j]
            ih1[j] = total
            sums = jnp.where(
                lane == j, jnp.sum(total * cot[i, j : j + 1, :], axis=1, keepdims=True), sums
            )
        so_out[i] = sums
        return unused

    lax.fori_loop(0, rows, cols_done, 0)
    hg_out[...] = jnp.exp(hl[...]) * dot(part[...].reshape(rows * cols, channels), gather)
    for c in started:
        c.wait_send()


def per_device(ha, wa, tokens, cotangent, state_in, state_out, width_decay, height_decay):
    rows, cols, channels = tokens.shape
    n = state_in.shape[2]
    groups = width_decay.shape[2]
    split = 1 if rows % wa == 0 else wa // rows
    chunk = channels // split
    per_w = rows * split // wa
    per_h = cols // ha
    vmem = pl.BlockSpec(memory_space=pltpu.VMEM)

    def room(*shape):
        return pltpu.VMEM(shape, F32)

    height = [
        room(cols, n, channels),
        room(ha, per_h, n, channels),
        room(ha, per_h, n, channels),
        room(cols, n, channels),
    ]
    width = [
        room(rows * split, n, chunk),
        room(wa, per_w, n, chunk),
        room(wa, per_w, n, chunk),
        room(rows * split, n, chunk),
    ]
    most = max(ha, wa)
    result = pl.pallas_call(
        functools.partial(kernel, ha, wa),
        out_shape=[
            jax.ShapeDtypeStruct((rows, cols, channels), F32),
            jax.ShapeDtypeStruct((rows, n, cols), F32),
            jax.ShapeDtypeStruct((rows, n, cols), F32),
            jax.ShapeDtypeStruct((rows * cols, groups), F32),
            jax.ShapeDtypeStruct((rows * cols, groups), F32),
        ],
        in_specs=[vmem] * 6,
        out_specs=[vmem] * 5,
        scratch_shapes=[room(rows, cols, channels) for _ in range(4)]
        + [
            room(rows * split, 1, chunk),
            room(cols, 1, channels),
            room(wa, per_w, 1, chunk),
            room(ha, per_h, 1, channels),
        ]
        + height
        + height
        + width
        + width
        + [
            room(rows, cols, n, channels),
            room(rows, cols, n, channels),
            room(rows, cols, channels),
            pltpu.SemaphoreType.DMA((10, most)),
            pltpu.SemaphoreType.DMA((10, most)),
        ],
        compiler_params=pltpu.CompilerParams(
            collective_id=0, has_side_effects=True, vmem_limit_bytes=48 * 1024 * 1024
        ),
        name="scan_back",
    )(
        tokens,
        cotangent,
        jnp.swapaxes(state_in, 1, 2),
        jnp.swapaxes(state_out, 1, 2),
        width_decay.reshape(rows * cols, groups),
        height_decay.reshape(rows * cols, groups),
    )
    return (
        result[0],
        jnp.swapaxes(result[1], 1, 2),
        jnp.swapaxes(result[2], 1, 2),
        result[3].reshape(rows, cols, groups),
        result[4].reshape(rows, cols, groups),
    )


def solution(mesh):
    spec = P("ha", "wa", None)
    return jax.shard_map(
        functools.partial(per_device, mesh.shape["ha"], mesh.shape["wa"]),
        mesh=mesh,
        in_specs=(spec,) * 6,
        out_specs=(spec,) * 5,
        check_vma=False,
    )
```

```python
import functools

import jax
import jax.numpy as jnp
from jax import lax
from jax.experimental import pallas as pl
from jax.experimental.pallas import tpu as pltpu
from jax.sharding import PartitionSpec as P

MESH = pl.DeviceIdType.MESH
F32 = jnp.float32


def kernel(
    ha,
    wa,
    x_in,
    cot_in,
    bt,
    ct,
    wl,
    hl,
    tok_out,
    in_out,
    so_out,
    wg_out,
    hg_out,
    x,
    cot,
    wr,
    hr,
    pw,
    ph,
    rpw,
    rph,
    eh0,
    rh0,
    oh0,
    ih0,
    eh1,
    rh1,
    oh1,
    ih1,
    ew0,
    rw0,
    ow0,
    iw0,
    ew1,
    rw1,
    ow1,
    iw1,
    states,
    grads,
    part,
    send,
    recv,
):
    rows, cols, channels = x_in.shape
    n = bt.shape[1]
    groups = wl.shape[1]
    gw = channels // groups
    split = ew0.shape[0] // rows
    chunk = channels // split
    per_w = rows * split // wa
    per_h = cols // ha
    me_h = lax.axis_index("ha")
    me_w = lax.axis_index("wa")
    place = {"ha": (me_h, ha, per_h), "wa": (me_w, wa, per_w)}

    barrier = pltpu.get_barrier_semaphore()
    for axis in ("ha", "wa"):
        me, count, per = place[axis]
        for d in range(1, count):
            pl.semaphore_signal(
                barrier, inc=1, device_id={axis: lax.rem(me + d, count)}, device_id_type=MESH
            )

    def copies(axis, k, source, target):
        me, count, per = place[axis]
        made = []
        for d in range(1, count):
            peer = lax.rem(me + d, count)
            made.append(
                pltpu.make_async_remote_copy(
                    src_ref=source(peer, per),
                    dst_ref=target(me, per),
                    send_sem=send.at[k, d],
                    recv_sem=recv.at[k, d],
                    device_id={axis: peer},
                    device_id_type=MESH,
                )
            )
        return made

    started = []

    def scatter(axis, k, ends, got):
        made = copies(
            axis, k, lambda peer, per: ends.at[pl.ds(peer * per, per)], lambda me, per: got.at[me]
        )
        for c in made:
            c.start()
        me, count, per = place[axis]
        got[me] = ends[pl.ds(me * per, per)]
        started.extend(made)
        return made

    def give_back(axis, k, result, first):
        made = copies(
            axis, k, lambda peer, per: result.at[peer], lambda me, per: first.at[pl.ds(me * per, per)]
        )
        for c in made:
            c.start()
        me, count, per = place[axis]
        first[pl.ds(me * per, per)] = result[me]
        started.extend(made)
        return made

    def arrive(made):
        for c in made:
            c.wait_recv()

    def put(buffer, i, value):
        for q in range(split):
            buffer[i * split + q] = value[:, q * chunk : (q + 1) * chunk]

    def take(buffer, i):
        return jnp.concatenate([buffer[i * split + q] for q in range(split)], axis=1)

    def chain(axis, got, product, result, backward):
        me, count, per = place[axis]
        order = range(count - 1, -1, -1) if backward else range(count)
        for p in range(per):
            current = jnp.zeros(got.shape[2:], F32)
            for s in order:
                result[s, p] = current
                current = product[s, p] * current + got[s, p]

    def onehot(shape, group_dim):
        g = lax.broadcasted_iota(jnp.int32, shape, group_dim) * gw
        c = lax.broadcasted_iota(jnp.int32, shape, 1 - group_dim)
        return jnp.where((c >= g) & (c < g + gw), 1.0, 0.0).astype(F32)

    def dot(a, b):
        return jnp.dot(a, b, precision=lax.Precision.HIGHEST, preferred_element_type=F32)

    spread = onehot((groups, channels), 0)
    hr[...] = dot(jnp.exp(hl[...]), spread).reshape(rows, cols, channels)
    wr[...] = dot(jnp.exp(wl[...]), spread).reshape(rows, cols, channels)
    x[...] = x_in[...].astype(F32)
    cot[...] = cot_in[...].astype(F32)
    whole = hr[0]
    for i in range(1, rows):
        whole = whole * hr[i]
    for j in range(cols):
        ph[j] = whole[j : j + 1]
    for i in range(rows):
        one = wr[i, 0:1, :]
        for j in range(1, cols):
            one = one * wr[i, j : j + 1, :]
        put(pw, i, one)

    eh0[...] = jnp.zeros_like(eh0)
    eh1[...] = jnp.zeros_like(eh1)

    def col_ends(t, unused):
        i = rows - 1 - t
        columns = ct[i]
        for j in range(cols):
            total = columns[:, j : j + 1] * cot[i, j : j + 1, :] + eh0[j]
            eh0[j] = hr[i, j : j + 1, :] * total
        return unused

    lax.fori_loop(0, rows, col_ends, 0)

    pl.semaphore_wait(barrier, ha + wa - 2)
    got_ph = scatter("ha", 8, ph, rph)
    out_h0 = scatter("ha", 0, eh0, rh0)

    def row_ends(i, unused):
        columns = bt[i]
        carry = columns[:, 0:1] * x[i, 0:1, :]
        for j in range(1, cols):
            carry = wr[i, j : j + 1, :] * carry + columns[:, j : j + 1] * x[i, j : j + 1, :]
        put(ew0, i, carry)
        return unused

    lax.fori_loop(0, rows, row_ends, 0)
    got_pw = scatter("wa", 9, pw, rpw)
    out_w0 = scatter("wa", 1, ew0, rw0)

    arrive(got_pw)
    arrive(out_w0)
    chain("wa", rw0, rpw, ow0, False)
    back_w0 = give_back("wa", 5, ow0, iw0)
    arrive(got_ph)
    arrive(out_h0)
    chain("ha", rh0, rph, oh0, True)
    back_h0 = give_back("ha", 4, oh0, ih0)

    arrive(back_w0)

    def forward(i, unused):
        columns = bt[i]
        carry = take(iw0, i)
        for j in range(cols):
            carry = wr[i, j : j + 1, :] * carry + columns[:, j : j + 1] * x[i, j : j + 1, :]
            states[i, j] = carry
            eh1[j] = hr[i, j : j + 1, :] * eh1[j] + carry
        return unused

    lax.fori_loop(0, rows, forward, 0)
    out_h1 = scatter("ha", 3, eh1, rh1)

    arrive(back_h0)

    def backward(t, unused):
        i = rows - 1 - t
        columns = ct[i]
        carry = jnp.zeros((n, channels), F32)
        for j in range(cols - 1, -1, -1):
            grad = columns[:, j : j + 1] * cot[i, j : j + 1, :] + ih0[j]
            grads[i, j] = grad
            ih0[j] = hr[i, j : j + 1, :] * grad
            carry = wr[i, j : j + 1, :] * (grad + carry)
        put(ew1, i, carry)
        return unused

    lax.fori_loop(0, rows, backward, 0)
    out_w1 = scatter("wa", 2, ew1, rw1)

    arrive(out_h1)
    chain("ha", rh1, rph, oh1, False)
    back_h1 = give_back("ha", 7, oh1, ih1)
    arrive(out_w1)
    chain("wa", rw1, rpw, ow1, True)
    back_w1 = give_back("wa", 6, ow1, iw1)

    lane = lax.broadcasted_iota(jnp.int32, (n, cols), 1)
    arrive(back_w1)

    def rows_done(i, unused):
        columns = bt[i]
        carry = take(iw1, i)
        sums = jnp.zeros((n, cols), F32)
        for j in range(cols - 1, -1, -1):
            grad = grads[i, j] + carry
            carry = wr[i, j : j + 1, :] * grad
            earlier = states[i, j - 1] if j else take(iw0, i)
            part[i, j : j + 1, :] = jnp.sum(grad * earlier, axis=0, keepdims=True)
            tok_out[i, j : j + 1, :] = jnp.sum(grad * columns[:, j : j + 1], axis=0, keepdims=True)
            sums = jnp.where(
                lane == j, jnp.sum(grad * x[i, j : j + 1, :], axis=1, keepdims=True), sums
            )
        in_out[i] = sums
        return unused

    lax.fori_loop(0, rows, rows_done, 0)
    gather = onehot((channels, groups), 1)
    wg_out[...] = jnp.exp(wl[...]) * dot(part[...].reshape(rows * cols, channels), gather)

    arrive(back_h1)

    def cols_done(i, unused):
        sums = jnp.zeros((n, cols), F32)
        for j in range(cols):
            earlier = ih1[j]
            part[i, j : j + 1, :] = jnp.sum(grads[i, j] * earlier, axis=0, keepdims=True)
            total = hr[i, j : j + 1, :] * earlier + states[i, j]
            ih1[j] = total
            sums = jnp.where(
                lane == j, jnp.sum(total * cot[i, j : j + 1, :], axis=1, keepdims=True), sums
            )
        so_out[i] = sums
        return unused

    lax.fori_loop(0, rows, cols_done, 0)
    hg_out[...] = jnp.exp(hl[...]) * dot(part[...].reshape(rows * cols, channels), gather)
    for c in started:
        c.wait_send()


def per_device(ha, wa, tokens, cotangent, state_in, state_out, width_decay, height_decay):
    rows, cols, channels = tokens.shape
    n = state_in.shape[2]
    groups = width_decay.shape[2]
    split = 1 if rows % wa == 0 else wa // rows
    chunk = channels // split
    per_w = rows * split // wa
    per_h = cols // ha
    vmem = pl.BlockSpec(memory_space=pltpu.VMEM)

    def room(*shape):
        return pltpu.VMEM(shape, F32)

    height = [
        room(cols, n, channels),
        room(ha, per_h, n, channels),
        room(ha, per_h, n, channels),
        room(cols, n, channels),
    ]
    width = [
        room(rows * split, n, chunk),
        room(wa, per_w, n, chunk),
        room(wa, per_w, n, chunk),
        room(rows * split, n, chunk),
    ]
    most = max(ha, wa)
    result = pl.pallas_call(
        functools.partial(kernel, ha, wa),
        out_shape=[
            jax.ShapeDtypeStruct((rows, cols, channels), F32),
            jax.ShapeDtypeStruct((rows, n, cols), F32),
            jax.ShapeDtypeStruct((rows, n, cols), F32),
            jax.ShapeDtypeStruct((rows * cols, groups), F32),
            jax.ShapeDtypeStruct((rows * cols, groups), F32),
        ],
        in_specs=[vmem] * 6,
        out_specs=[vmem] * 5,
        scratch_shapes=[room(rows, cols, channels) for _ in range(4)]
        + [
            room(rows * split, 1, chunk),
            room(cols, 1, channels),
            room(wa, per_w, 1, chunk),
            room(ha, per_h, 1, channels),
        ]
        + height
        + height
        + width
        + width
        + [
            room(rows, cols, n, channels),
            room(rows, cols, n, channels),
            room(rows, cols, channels),
            pltpu.SemaphoreType.DMA((10, most)),
            pltpu.SemaphoreType.DMA((10, most)),
        ],
        compiler_params=pltpu.CompilerParams(
            collective_id=0, has_side_effects=True, vmem_limit_bytes=48 * 1024 * 1024
        ),
        name="scan_back",
    )(
        tokens,
        cotangent,
        jnp.swapaxes(state_in, 1, 2),
        jnp.swapaxes(state_out, 1, 2),
        width_decay.reshape(rows * cols, groups),
        height_decay.reshape(rows * cols, groups),
    )
    return (
        result[0],
        jnp.swapaxes(result[1], 1, 2),
        jnp.swapaxes(result[2], 1, 2),
        result[3].reshape(rows, cols, groups),
        result[4].reshape(rows, cols, groups),
    )


def solution(mesh):
    spec = P("ha", "wa", None)
    return jax.shard_map(
        functools.partial(per_device, mesh.shape["ha"], mesh.shape["wa"]),
        mesh=mesh,
        in_specs=(spec,) * 6,
        out_specs=(spec,) * 5,
        check_vma=False,
    )
```
